32 devices in a mesh: grp: 2 (over x), seq: 16 (over z, y, core).
Axes of the slice: x: 2, y: 2, z: 4, core: 2. Of those that a mesh axis runs over, the one named last changes fastest.
Arguments:
- queries: bfloat16 [8192, 8192], P(('grp', 'seq')), parts along dimension 0, may hold values from -6 to 6
- keys_in: bfloat16 [8192, 8192], P(('grp', 'seq')), parts along dimension 0, may hold values from -0.375 to 0.375
- values_in: bfloat16 [8192, 8192], P(('grp', 'seq')), parts along dimension 0, may hold values from -6 to 6
- log_decay: bfloat16 [8192, 64], P(('grp', 'seq')), parts along dimension 0, may hold values from -2 to 0, as said below
- gate_logits: bfloat16 [8192, 8192], P(('grp', 'seq')), parts along dimension 0, may hold values from -6 to 6
- norm_gain: float32 [8192], replicated, may hold values from 0.1 to 1.9
- doc_lengths: int32 [16], P('grp'), parts along dimension 0, may hold values from 1 to 2048, 4096 in all
Outputs:
- attended: bfloat16 [8192, 8192], P(('grp', 'seq')), parts along dimension 0
- final_state: float32 [128, 128, 128], P(('grp', 'seq')), parts along dimension 0
The draws below stay inside these ranges and needn't reach their ends.
There are 2 independent parts, one for each index of `grp`. The reference program is written for one: setup_inputs(seed, part) draws one part's arguments, and reference() takes and returns one part's arrays. A program takes and returns all parts, laid end to end along the dimension named above; an argument that names none is the same for every part. Nothing has to cross between parts.
Inputs may be any that keep to these rules, and one draw needn't show every extreme that they name: log_decay is negative. `doc_lengths`: the 8 lengths are positive and sum to 4096.
All inputs are finite; a program needn't handle non-finite values.
Results may differ from the reference program's by a relative error of at most 0.0049.
Values may be sent and summed in bfloat16 or wider, within the bound.
A program may use at most 320 MiB of HBM per device.

```python
import math
import jax
import jax.numpy as jnp
import numpy as np
from jax import lax

HEADS = 64
HEAD_DIM = 128
SPAN = 256
DOCS = 8
TOK_DEV = 256
PACKED_TOKENS = 4096


def draw_log_decay(key, part):
    fast_share = 0.5
    fast = jax.random.uniform(jax.random.fold_in(key, 11), (HEADS,)) < fast_share
    fast_rate = jax.random.uniform(jax.random.fold_in(key, 12), (HEADS,), minval=1.0 / 40.0, maxval=1.0 / 25.0)
    slow_rate = jax.random.uniform(jax.random.fold_in(key, 13), (HEADS,), minval=0.1, maxval=0.3) * 2.302585 / PACKED_TOKENS
    decay_rate = jnp.where(fast, fast_rate, slow_rate)
    token_decay_factor = jax.random.uniform(jax.random.fold_in(key, 14), (PACKED_TOKENS, HEADS), minval=0.5, maxval=1.5)
    block_decay_factor = jax.random.uniform(jax.random.fold_in(key, 15), (PACKED_TOKENS // TOK_DEV, 1, HEADS), minval=0.5, maxval=1.5)
    block_decay_factor = jnp.broadcast_to(block_decay_factor, (PACKED_TOKENS // TOK_DEV, TOK_DEV, HEADS)).reshape(PACKED_TOKENS, HEADS)
    spike_positions = jax.random.randint(jax.random.fold_in(key, 16), (2,), 0, PACKED_TOKENS)
    retention = jax.random.uniform(jax.random.fold_in(key, 17), (2, HEADS), minval=0.5, maxval=0.8)
    spike_flags = (jnp.arange(PACKED_TOKENS)[:, None] == spike_positions[None, :]).astype(jnp.float32)
    spike_log_decay = jnp.dot(spike_flags, jnp.log(retention))
    return (-decay_rate[None, :] * token_decay_factor * block_decay_factor + spike_log_decay).astype(jnp.bfloat16)


def block_levels(rng, shape, shards, low, largest):
    def one(axis_at, blocks):
        heights = jax.random.uniform(jax.random.fold_in(jax.random.fold_in(rng, 6), axis_at), (blocks,), jnp.float32, low / len(shards), largest / len(shards))
        return jnp.repeat(jnp.exp(heights), shape[axis_at] // blocks).reshape((-1,) + (1,) * (len(shape) - axis_at - 1))

    loudness = one(*shards[0])
    for cut in shards[1:]:
        loudness = loudness * one(*cut)
    return loudness


def profile(amount, total, bound, slope):
    portions = [(1 << 20) // math.isqrt(grade ** slope) + 1 for grade in range(2, amount + 1)]
    spare, counts = total - bound - (amount - 1), [1] * (amount - 1)
    while spare > 0:
        free = [i for i in range(amount - 1) if counts[i] < bound]
        pool, left = sum([portions[i] for i in free]), spare
        for i in free:
            extra = min(bound - counts[i], max(1, left * portions[i] // pool), spare)
            counts[i] = counts[i] + extra
            spare = spare - extra
    return np.array([bound] + counts)


def ragged(own_key, amount, total, most, skew):
    if amount == 2:
        one = jax.random.randint(own_key, (), max(1, total - most), min(most, total - 1) + 1)
        return jnp.stack([one, total - one])
    sizes = jnp.asarray(profile(amount, total, most, skew), jnp.int32)
    couples = (amount - 1) // 2
    donor, taker = sizes[1:1 + 2 * couples:2], sizes[2:2 + 2 * couples:2]
    slack = jnp.minimum(donor - 1, most - taker)
    moved = jax.random.randint(jax.random.fold_in(own_key, 1), (couples,), 0, 1 << 20) % (slack + 1)
    sizes = sizes.at[1:1 + 2 * couples:2].set(donor - moved).at[2:2 + 2 * couples:2].set(taker + moved)
    return sizes[jax.random.permutation(jax.random.fold_in(own_key, 2), amount)]


def noise(rng, dims, width, limit, split=(), kind=jnp.bfloat16):
    result = jax.random.normal(rng, dims, jnp.float32) * width
    if len(split) > 0:
        result = block_levels(rng, dims, split, -0.22, 0.18) * result
    return jnp.clip(result, min=-limit, max=limit).astype(kind)


def setup_inputs(seed: int = 0, part: int = 0) -> dict:
    streams_of = jax.random.split(jax.random.key(seed), 8)
    part_splits = jax.random.split(jax.random.fold_in(streams_of[7], part), 8)
    queries = noise(part_splits[0], (PACKED_TOKENS, HEADS * HEAD_DIM), 1.0, 6.0, ((0, 16),))
    keys_in = noise(part_splits[1], (PACKED_TOKENS, HEADS * HEAD_DIM), 0.0625, 0.375, ((0, 16),))
    values_in = noise(part_splits[2], (PACKED_TOKENS, HEADS * HEAD_DIM), 1.0, 6.0, ((0, 16),))
    log_decay = draw_log_decay(jax.random.fold_in(jax.random.fold_in(streams_of[7], part), 71), part)
    gate_logits = noise(part_splits[4], (PACKED_TOKENS, HEADS * HEAD_DIM), 1.0, 6.0, ((0, 16),))
    norm_gain = jnp.clip(1.0 + 0.18 * jax.random.normal(streams_of[5], (HEADS * HEAD_DIM,), jnp.float32), 0.1, 1.9)
    doc_lengths = ragged(part_splits[6], DOCS, PACKED_TOKENS, PACKED_TOKENS // 2, 2).astype(jnp.int32)
    return {"queries": queries, "keys_in": keys_in, "values_in": values_in, "log_decay": log_decay, "gate_logits": gate_logits, "norm_gain": norm_gain, "doc_lengths": doc_lengths}


EPS = 1e-05

def doc_index(doc_lengths, positions):
    doc_ends = jnp.cumsum(doc_lengths).astype(jnp.int32)
    return lax.optimization_barrier(jnp.sum((positions[:, None] >= doc_ends[None, :]).astype(jnp.int32), axis=1)).astype(jnp.int32)

def reference(queries, keys_in, values_in, log_decay, gate_logits, norm_gain, doc_lengths):
    spans = PACKED_TOKENS // SPAN
    positions = jnp.arange(PACKED_TOKENS, dtype=jnp.int32)
    documents = doc_index(doc_lengths, positions).reshape(spans, SPAN)
    before = doc_index(doc_lengths, positions - 1).reshape(spans, SPAN)[:, 0]
    span_shape = (spans, SPAN, HEADS, HEAD_DIM)
    query_rows = queries.reshape(span_shape)
    key_rows = keys_in.reshape(span_shape)
    value_rows = values_in.reshape(span_shape)
    decay_rows = log_decay.astype(jnp.float32).reshape(spans, SPAN, HEADS)
    causal = jnp.arange(SPAN)[:, None] >= jnp.arange(SPAN)[None, :]

    def advance(state, batch_item):
        query_blk, key_blk, value_blk, decay_blk, doc_blk, prior_doc = batch_item
        cumulative = jnp.cumsum(decay_blk, axis=0)
        allowed = causal & (doc_blk[:, None] == doc_blk[None, :])
        cumul_heads = cumulative.T
        spread_log = jnp.where(allowed[None], cumul_heads[:, :, None] - cumul_heads[:, None, :], 0.0)
        decay_grid = jnp.where(allowed[None], jnp.exp(spread_log), 0.0)
        query_f = query_blk.astype(jnp.float32)
        key_f = key_blk.astype(jnp.float32)
        value_f = value_blk.astype(jnp.float32)
        scores = jnp.einsum('ihd,jhd->hij', query_f, key_f)
        weights = lax.optimization_barrier((scores * decay_grid).astype(jnp.bfloat16)).astype(jnp.float32)
        inside = jnp.einsum('hij,jhd->ihd', weights, value_f)
        carried = (doc_blk == prior_doc).astype(jnp.float32)
        across = jnp.einsum('ihd,hde->ihe', query_f, state, precision=lax.Precision.HIGHEST)
        across = across * (carried[:, None] * jnp.exp(cumulative))[:, :, None]
        closing_doc = (doc_blk == doc_blk[-1]).astype(jnp.float32)
        key_weight = closing_doc[:, None] * jnp.exp(cumulative[-1][None, :] - cumulative)
        weighted = lax.optimization_barrier((key_f * key_weight[:, :, None]).astype(jnp.bfloat16)).astype(jnp.float32)
        update = jnp.einsum('jhd,jhe->hde', weighted, value_f)
        factor = carried[-1] * jnp.exp(cumulative[-1])
        new_state = factor[:, None, None] * state + update
        return (new_state, inside + across)
    initial = jnp.zeros((HEADS, HEAD_DIM, HEAD_DIM), jnp.float32)
    final_state, outputs = lax.scan(advance, initial, (query_rows, key_rows, value_rows, decay_rows, documents, before))
    mixed = outputs.reshape(PACKED_TOKENS, HEADS * HEAD_DIM)
    inverse_rms = lax.rsqrt(lax.optimization_barrier(jnp.mean(mixed * mixed, axis=1, keepdims=True)) + EPS)
    gated = mixed * inverse_rms * norm_gain[None, :] * jax.nn.sigmoid(gate_logits.astype(jnp.float32))
    return (gated.astype(jnp.bfloat16), final_state)
```

```python
import functools
import math

import jax
import jax.numpy as jnp
from jax import lax
from jax.experimental import pallas as pl
from jax.experimental.pallas import tpu as pltpu
from jax.sharding import PartitionSpec as P

EPS = 1e-05
D = 128
GROUP = 4
CHUNKS = 8
F32, BF16 = jnp.float32, jnp.bfloat16
MESH = pl.DeviceIdType.MESH


def dot(a, b, dims):
    return lax.dot_general(a, b, (dims, ((), ())), preferred_element_type=F32)


def kernel(
    n, heads, chunks,
    q_hbm, k_hbm, v_hbm, g_hbm, ld_ref, gain_ref, docs_ref,
    out_hbm, fin_ref,
    q_s, k_s, v_s, g_s, gate_s, mix_s, ssq_s, pen_s, cumt_s, cumc_s, kw_s, lead_s,
    fac_own, fac_s, u_own, u_core, u_mine, u_send, u_pair, s_in, s_out, e_send, e_half, x_send, ent, fin_s,
    load_sem, out_sem, fac_ss, fac_rs, core_ss, core_rs, pair_ss, pair_rs, z_ss, z_rs, e_ss, e_rs,
    x_ss, x_rs, f_ss, f_rs, f_ls,
):
    tok = q_hbm.shape[0]
    hc = heads // chunks
    half = hc // 2
    w = half // 2
    planes = n // GROUP
    hn = heads // n
    g = math.gcd(w, hn)
    me = lax.axis_index("seq")
    plane = me // GROUP
    r = me % GROUP
    y = r // 2
    c = r % 2
    core_peer = plane * GROUP + y * 2 + (1 - c)
    pair_peer = plane * GROUP + (1 - y) * 2 + c

    def send(src, dst, ss, rs, dev):
        return pltpu.make_async_remote_copy(
            src_ref=src, dst_ref=dst, send_sem=ss, recv_sem=rs,
            device_id={"seq": dev}, device_id_type=MESH,
        )

    barrier = pltpu.get_barrier_semaphore()

    def greet(i, carry):
        pl.semaphore_signal(barrier, inc=1, device_id={"seq": (me + i) % n}, device_id_type=MESH)
        return carry

    lax.fori_loop(1, n, greet, 0)

    def cols(j):
        return pl.ds(pl.multiple_of(j * (hc * D), hc * D), hc * D)

    def load(which, hbm, vm, j):
        return pltpu.make_async_copy(hbm.at[:, cols(j)], vm.at[:, cols(j)], load_sem.at[which, j])

    loads = ((k_hbm, k_s), (v_hbm, v_s), (q_hbm, q_s), (g_hbm, g_s))

    def start_kv(j, carry):
        load(0, k_hbm, k_s, j).start()
        load(1, v_hbm, v_s, j).start()
        return carry

    def start_qg(j, carry):
        load(2, q_hbm, q_s, j).start()
        load(3, g_hbm, g_s, j).start()
        return carry

    lax.fori_loop(0, chunks, start_kv, 0)
    lax.fori_loop(0, chunks, start_qg, 0)

    n_docs = docs_ref.shape[0]
    rows = lax.broadcasted_iota(jnp.int32, (tok, tok), 0)
    lanes = lax.broadcasted_iota(jnp.int32, (tok, tok), 1)
    base = me * tok
    doc_col = jnp.zeros((tok, tok), jnp.int32)
    doc_row = jnp.zeros((tok, tok), jnp.int32)
    before = jnp.int32(0)
    last = jnp.int32(0)
    end = jnp.int32(0)
    for d in range(n_docs):
        end = end + docs_ref[d]
        doc_col = doc_col + jnp.where(rows + base >= end, 1, 0)
        doc_row = doc_row + jnp.where(lanes + base >= end, 1, 0)
        before = before + jnp.where(base - 1 >= end, 1, 0)
        last = last + jnp.where(base + tok - 1 >= end, 1, 0)
    causal = rows >= lanes
    pen_s[...] = jnp.where(causal & (doc_col == doc_row), 0.0, -1e30).astype(F32)
    tri = jnp.where(causal, 1.0, 0.0).astype(BF16)
    ld = ld_ref[...]
    cum = dot(tri, ld, ((1,), (0,)))
    cumt = dot(ld, tri, ((0,), (1,)))
    cumt_s[...] = cumt
    carried = jnp.where(doc_col[:, :heads] == before, 1.0, 0.0).astype(F32)
    closing = jnp.where(doc_col[:, :heads] == last, 1.0, 0.0).astype(F32)
    lead = carried * jnp.exp(cum)
    kw = closing * jnp.exp(cum[tok - 1:tok, :] - cum)
    for j in range(chunks):
        at = slice(j * hc, (j + 1) * hc)
        cumc_s[j] = cum[:, at]
        lead_s[j] = lead[:, at]
        kw_s[j] = kw[:, at]
    own_f = jnp.where(last == before, 1.0, 0.0).astype(F32) * jnp.exp(
        jnp.broadcast_to(cumt[:, tok - 1:tok], (heads, D))
    )
    fac_own[...] = own_f
    fac_s[r] = own_f

    @pl.when(plane == 0)
    def _():
        s_in[...] = jnp.zeros_like(s_in)

    def lane(t):
        return slice(t * D, (t + 1) * D)

    def hcol(j, t):
        return pl.ds(pl.multiple_of(j * (hc * D) + t * D, D), D)

    def updates(j):
        load(0, k_hbm, k_s, j).wait()
        load(1, v_hbm, v_s, j).wait()
        kwj = kw_s[j]
        for t in range(hc):
            kk = k_s[:, hcol(j, t)].astype(F32)
            wk = (kk * kwj[:, t:t + 1]).astype(BF16)
            up = dot(wk, v_s[:, hcol(j, t)], ((0,), (0,)))
            u_own[j, t // half, (t % half) // w, t % w] = up.astype(BF16)

    def frow(slot, h):
        return fac_s[slot, pl.ds(h, 1), :]

    def core_copy(j):
        return send(u_own.at[j, 1 - c], u_core.at[j], core_ss.at[j], core_rs.at[j], core_peer)

    def pair_copy(j):
        return send(u_send.at[j], u_pair.at[j], pair_ss.at[j], pair_rs.at[j], pair_peer)

    def combine(j):
        core_copy(j).wait_recv()
        for k in range(w):
            for mine in (True, False):
                yo = y if mine else 1 - y
                h = j * hc + c * half + yo * w + k
                f1 = frow(2 * y + 1, h)
                fa = jnp.where(c == 0, f1, 1.0)
                fb = jnp.where(c == 0, 1.0, f1)
                val = fa * u_own[j, c, yo, k].astype(F32) + fb * u_core[j, yo, k].astype(F32)
                if mine:
                    u_mine[j, k] = val
                else:
                    u_send[j, k] = val.astype(BF16)
        pair_copy(j).start()

    def z_copy(j):
        return send(s_out.at[j], s_in.at[j], z_ss.at[j], z_rs.at[j], (me + GROUP) % n)

    def e_copy(j):
        return send(e_send.at[j], e_half.at[j, y], e_ss.at[j], e_rs.at[j], pair_peer)

    def fin_place(j, s):
        h0 = j * hc + c * half + y * w + s * g
        return h0 // hn, h0 % hn

    def fin_copy(j, s):
        dev, off = fin_place(j, s)
        return send(
            s_out.at[j, pl.ds(s * g, g)], fin_s.at[pl.ds(off, g)],
            f_ss.at[j, s], f_rs.at[off // g], dev,
        )

    def fin_local(j, s):
        _, off = fin_place(j, s)
        return pltpu.make_async_copy(s_out.at[j, pl.ds(s * g, g)], fin_s.at[pl.ds(off, g)], f_ls)

    def chain(j):
        pair_copy(j).wait_recv()

        @pl.when(plane > 0)
        def _():
            z_copy(j).wait_recv()

        for k in range(w):
            h = j * hc + c * half + y * w + k
            f01 = frow(0, h) * frow(1, h)
            f23 = frow(2, h) * frow(3, h)
            mine = u_mine[j, k]
            other = u_pair[j, k].astype(F32)
            entry = s_in[j, k].astype(F32)
            mid = f01 * entry + jnp.where(y == 0, mine, other)
            s_out[j, k] = (f23 * mid + jnp.where(y == 0, other, mine)).astype(BF16)
            e_send[j, k] = jnp.where(y == 0, mid, entry).astype(BF16)
            e_half[j, y, k] = jnp.where(y == 0, entry, mid).astype(BF16)

        @pl.when(plane < planes - 1)
        def _():
            z_copy(j).start()

        e_copy(j).start()

        @pl.when(plane == planes - 1)
        def _():
            for s in range(w // g):
                dev, _off = fin_place(j, s)

                @pl.when(dev != me)
                def _():
                    fin_copy(j, s).start()

                @pl.when(dev == me)
                def _():
                    fin_local(j, s).start()
                    fin_local(j, s).wait()

    def inside(j):
        load(2, q_hbm, q_s, j).wait()
        load(3, g_hbm, g_s, j).wait()
        cj = cumc_s[j]
        blk = tok // 2
        for t in range(hc):
            row = cumt_s[pl.ds(j * hc + t, 1), :]
            for b in range(2):
                at = slice(b * blk, (b + 1) * blk)
                width = (b + 1) * blk
                scores = dot(q_s[at, hcol(j, t)], k_s[:width, hcol(j, t)], ((1,), (1,)))
                grid = jnp.exp((cj[at, t:t + 1] - row[:, :width]) + pen_s[at, :width])
                wt = (scores * grid).astype(BF16)
                mix_s[at, hcol(j, t)] = dot(wt, v_s[:width, hcol(j, t)], ((1,), (0,)))
            gate = g_s[:, hcol(j, t)].astype(F32)
            gate_s[:, hcol(j, t)] = gain_ref[:, hcol(j, t)] * jax.nn.sigmoid(gate)

    def x_copy(j):
        return send(x_send.at[j], ent.at[j, c], x_ss.at[j], x_rs.at[j], core_peer)

    def spread(j):
        e_copy(j).wait_recv()
        for yo in range(2):
            for k in range(w):
                h = j * hc + c * half + yo * w + k
                first = e_half[j, yo, k]
                u0 = jnp.where(c == 0, u_own[j, 0, yo, k], u_core[j, yo, k]).astype(F32)
                second = (frow(2 * y, h) * first.astype(F32) + u0).astype(BF16)
                ent[j, c, yo, k] = jnp.where(c == 0, first, second)
                x_send[j, yo, k] = jnp.where(c == 0, second, first)
        x_copy(j).start()

    def across(j):
        x_copy(j).wait_recv()
        lj = lead_s[j]
        acc = ssq_s[...]
        for t in range(hc):
            st = ent[j, t // half, (t % half) // w, t % w]
            mixed = mix_s[:, hcol(j, t)] + lj[:, t:t + 1] * dot(q_s[:, hcol(j, t)], st, ((1,), (0,)))
            acc = acc + mixed * mixed
            mix_s[:, hcol(j, t)] = mixed * gate_s[:, hcol(j, t)]
        ssq_s[...] = acc

    def fac_copy(d):
        return send(fac_own, fac_s.at[r], fac_ss.at[d - 1], fac_rs.at[d - 1], plane * GROUP + (r + d) % GROUP)

    updates(0)
    pl.semaphore_wait(barrier, n - 1)
    for d in range(1, GROUP):
        fac_copy(d).start()
    core_copy(0).start()
    ssq_s[...] = jnp.zeros_like(ssq_s)
    for d in range(1, GROUP):
        fac_copy(d).wait_recv()

    def first_pass(j, carry):
        updates(j)
        core_copy(j).start()
        combine(j - 1)
        return carry

    lax.fori_loop(1, chunks, first_pass, 0)
    combine(chunks - 1)

    def second_pass(j, carry):
        inside(j)
        chain(j)
        return carry

    lax.fori_loop(0, chunks, second_pass, 0)
    spread(0)

    def third_pass(j, carry):
        spread(j)
        across(j - 1)
        return carry

    lax.fori_loop(1, chunks, third_pass, 0)
    across(chunks - 1)

    inv = lax.rsqrt(jnp.sum(ssq_s[...], axis=1, keepdims=True) * (1.0 / (heads * D)) + EPS)

    def store(j):
        return pltpu.make_async_copy(g_s.at[:, cols(j)], out_hbm.at[:, cols(j)], out_sem.at[j])

    def finish(j, carry):
        for t in range(hc):
            g_s[:, hcol(j, t)] = (mix_s[:, hcol(j, t)] * inv).astype(BF16)
        store(j).start()
        return carry

    lax.fori_loop(0, chunks, finish, 0)

    for s in range(hn // g):
        h0 = me * hn + s * g
        pos = h0 % hc
        src = (planes - 1) * GROUP + ((pos % half) // w) * 2 + pos // half

        @pl.when(src != me)
        def _():
            send(
                s_out.at[0, pl.ds(0, g)], fin_s.at[pl.ds(s * g, g)], f_ss.at[0, 0], f_rs.at[s], core_peer
            ).wait_recv()

    fin_ref[...] = fin_s[...].astype(F32)

    for d in range(1, GROUP):
        fac_copy(d).wait_send()

    def drain(j, carry):
        core_copy(j).wait_send()
        pair_copy(j).wait_send()
        e_copy(j).wait_send()
        x_copy(j).wait_send()
        store(j).wait()

        @pl.when(plane < planes - 1)
        def _():
            z_copy(j).wait_send()

        @pl.when(plane == planes - 1)
        def _():
            for s in range(w // g):
                dev, _off = fin_place(j, s)

                @pl.when(dev != me)
                def _():
                    fin_copy(j, s).wait_send()

        return carry

    lax.fori_loop(0, chunks, drain, 0)


def shards(n, queries, keys_in, values_in, log_decay, gate_logits, norm_gain, doc_lengths):
    tok, width = queries.shape
    heads = width // D
    chunks = CHUNKS
    hc = heads // chunks
    half = hc // 2
    w = half // 2
    hn = heads // n
    g = math.gcd(w, hn)
    vm = pltpu.VMEM
    dma = pltpu.SemaphoreType.DMA
    anyspace = pl.BlockSpec(memory_space=pl.ANY)
    vspec = pl.BlockSpec(memory_space=pltpu.VMEM)
    part = vm((chunks, w, D, D), BF16)
    scratch = [
        vm((tok, width), BF16), vm((tok, width), BF16), vm((tok, width), BF16), vm((tok, width), BF16),
        vm((tok, width), F32), vm((tok, width), F32), vm((tok, D), F32), vm((tok, tok), F32),
        vm((heads, tok), F32), vm((chunks, tok, hc), F32), vm((chunks, tok, hc), F32), vm((chunks, tok, hc), F32),
        vm((heads, D), F32), vm((GROUP, heads, D), F32),
        vm((chunks, 2, 2, w, D, D), BF16), vm((chunks, 2, w, D, D), BF16), vm((chunks, w, D, D), F32),
        part, part, part, part, part,
        vm((chunks, 2, w, D, D), BF16), vm((chunks, 2, w, D, D), BF16),
        vm((chunks, 2, 2, w, D, D), BF16), vm((hn, D, D), BF16),
        dma((4, chunks)), dma((chunks,)), dma((GROUP - 1,)), dma((GROUP - 1,)),
        dma((chunks,)), dma((chunks,)), dma((chunks,)), dma((chunks,)), dma((chunks,)), dma((chunks,)),
        dma((chunks,)), dma((chunks,)), dma((chunks,)), dma((chunks,)),
        dma((chunks, w // g)), dma((hn // g,)), dma,
    ]
    return pl.pallas_call(
        functools.partial(kernel, n, heads, chunks),
        out_shape=(
            jax.ShapeDtypeStruct((tok, width), BF16),
            jax.ShapeDtypeStruct((hn, D, D), F32),
        ),
        in_specs=[anyspace] * 4 + [vspec, vspec, pl.BlockSpec(memory_space=pltpu.SMEM)],
        out_specs=(anyspace, vspec),
        scratch_shapes=scratch,
        compiler_params=pltpu.CompilerParams(
            collective_id=0, has_side_effects=True, vmem_limit_bytes=60 * 1024 * 1024
        ),
    )(queries, keys_in, values_in, gate_logits, log_decay, norm_gain.reshape(1, width), doc_lengths)


def solution(mesh):
    rows = P(("grp", "seq"), None)
    return jax.shard_map(
        functools.partial(shards, mesh.shape["seq"]),
        mesh=mesh,
        in_specs=(rows, rows, rows, rows, rows, P(), P("grp")),
        out_specs=(rows, P(("grp", "seq"), None, None)),
        check_vma=False,
    )
```

```python
import functools
import math

import jax
import jax.numpy as jnp
from jax import lax
from jax.experimental import pallas as pl
from jax.experimental.pallas import tpu as pltpu
from jax.sharding import PartitionSpec as P

EPS = 1e-05
LOG2E = 1.4426950408889634
D = 128
GROUP = 4
CHUNKS = 8
INSIDE_LAG = 2
CHAIN_LAG = 4
HOP_LAG = 2
E_LAG = 4
X_LAG = 2
FINISH_PARTS = 4
F32, BF16 = jnp.float32, jnp.bfloat16
MESH = pl.DeviceIdType.MESH


def dot(a, b, dims):
    return lax.dot_general(a, b, (dims, ((), ())), preferred_element_type=F32)


def kernel(
    n, heads, chunks,
    q_hbm, k_hbm, v_hbm, g_hbm, ld_ref, gain_ref, docs_ref,
    mix_hbm, ssq_s, fin_s,
    mix_s, q_s, k_s, v_s, g_s, pen_s, cumt_s, cumc_s, coef_s,
    fac_own, fac_s, u_own, u_core, u_mine, u_send, u_pair, s_in, s_out, e_send, e_half, x_send, ent,
    load_sem, out_sem, fac_ss, fac_rs, core_ss, core_rs, pair_ss, pair_rs, z_ss, z_rs, e_ss, e_rs,
    x_ss, x_rs, f_ss, f_rs, f_ls,
):
    tok = q_hbm.shape[0]
    hc = heads // chunks
    half = hc // 2
    w = half // 2
    planes = n // GROUP
    hn = heads // n
    g = math.gcd(w, hn)
    me = lax.axis_index("seq")
    plane = me // GROUP
    r = me % GROUP
    y = r // 2
    c = r % 2
    core_peer = plane * GROUP + y * 2 + (1 - c)
    pair_peer = plane * GROUP + (1 - y) * 2 + c

    def send(src, dst, ss, rs, dev):
        return pltpu.make_async_remote_copy(
            src_ref=src, dst_ref=dst, send_sem=ss, recv_sem=rs,
            device_id={"seq": dev}, device_id_type=MESH,
        )

    barrier = pltpu.get_barrier_semaphore()

    def greet(i, carry):
        pl.semaphore_signal(barrier, inc=1, device_id={"seq": (me + i) % n}, device_id_type=MESH)
        return carry

    lax.fori_loop(1, n, greet, 0)

    def cols(j):
        return pl.ds(pl.multiple_of(j * (hc * D), hc * D), hc * D)

    def load(which, hbm, vm, j):
        return pltpu.make_async_copy(hbm.at[:, cols(j)], vm.at[:, cols(j)], load_sem.at[which, j])

    loads = ((k_hbm, k_s), (v_hbm, v_s), (q_hbm, q_s), (g_hbm, g_s))

    def start_kv(j, carry):
        load(0, k_hbm, k_s, j).start()
        load(1, v_hbm, v_s, j).start()
        return carry

    def start_qg(j, carry):
        load(2, q_hbm, q_s, j).start()
        load(3, g_hbm, g_s, j).start()
        return carry

    lax.fori_loop(0, chunks, start_kv, 0)
    lax.fori_loop(0, chunks, start_qg, 0)

    n_docs = docs_ref.shape[0]
    rows = lax.broadcasted_iota(jnp.int32, (tok, tok), 0)
    lanes = lax.broadcasted_iota(jnp.int32, (tok, tok), 1)
    base = me * tok
    doc_col = jnp.zeros((tok, tok), jnp.int32)
    doc_row = jnp.zeros((tok, tok), jnp.int32)
    before = jnp.int32(0)
    last = jnp.int32(0)
    end = jnp.int32(0)
    for d in range(n_docs):
        end = end + docs_ref[d]
        doc_col = doc_col + jnp.where(rows + base >= end, 1, 0)
        doc_row = doc_row + jnp.where(lanes + base >= end, 1, 0)
        before = before + jnp.where(base - 1 >= end, 1, 0)
        last = last + jnp.where(base + tok - 1 >= end, 1, 0)
    causal = rows >= lanes
    pen_s[...] = jnp.where(causal & (doc_col == doc_row), 0.0, -1e30).astype(F32)
    tri = jnp.where(causal, 1.0, 0.0).astype(BF16)
    ld = ld_ref[...]
    cum = dot(tri, ld, ((1,), (1,)))
    cumt = dot(ld, tri, ((1,), (1,)))
    cumt_s[...] = LOG2E * cumt
    carried = jnp.where(doc_col[:, :heads] == before, 1.0, 0.0).astype(F32)
    closing = jnp.where(doc_col[:, :heads] == last, 1.0, 0.0).astype(F32)
    lead = carried * jnp.exp(cum)
    kw = closing * jnp.exp(cum[tok - 1:tok, :] - cum)
    for j in range(chunks):
        at = slice(j * hc, (j + 1) * hc)
        coef_s[j, :, 0:hc] = lead[:, at]
        coef_s[j, :, hc:2 * hc] = kw[:, at]
    for i in range(2 * chunks):
        cumc_s[i] = LOG2E * cum[:, i * half:(i + 1) * half]
    own_f = jnp.where(last == before, 1.0, 0.0).astype(F32) * jnp.exp(
        jnp.broadcast_to(cumt[:, tok - 1:tok], (heads, D))
    )
    fac_own[...] = own_f
    fac_s[r] = own_f

    @pl.when(plane == 0)
    def _():
        s_in[...] = jnp.zeros_like(s_in)

    def lane(t):
        return slice(t * D, (t + 1) * D)

    def hcol(j, t):
        return pl.ds(pl.multiple_of(j * (hc * D) + t * D, D), D)

    def updates(j):
        load(0, k_hbm, k_s, j).wait()
        load(1, v_hbm, v_s, j).wait()
        kwj = coef_s[j, :, hc:2 * hc]
        for t in range(hc):
            kk = k_s[:, hcol(j, t)].astype(F32)
            wk = (kk * kwj[:, t:t + 1]).astype(BF16)
            up = dot(wk, v_s[:, hcol(j, t)], ((0,), (0,)))
            u_own[j, t // half, (t % half) // w, t % w] = up.astype(BF16)

    def frow(slot, h):
        return fac_s[slot, pl.ds(h, 1), :]

    def core_copy(j):
        return send(u_own.at[j, 1 - c], u_core.at[j], core_ss.at[j], core_rs.at[j], core_peer)

    def pair_copy(j):
        return send(u_send.at[j], u_pair.at[j], pair_ss.at[j], pair_rs.at[j], pair_peer)

    def combine(j):
        core_copy(j).wait_recv()
        for k in range(w):
            for mine in (True, False):
                yo = y if mine else 1 - y
                h = j * hc + c * half + yo * w + k
                f1 = frow(2 * y + 1, h)
                fa = jnp.where(c == 0, f1, 1.0)
                fb = jnp.where(c == 0, 1.0, f1)
                val = fa * u_own[j, c, yo, k].astype(F32) + fb * u_core[j, yo, k].astype(F32)
                if mine:
                    u_mine[j, k] = val
                else:
                    u_send[j, k] = val.astype(BF16)
        pair_copy(j).start()

    def z_copy(j):
        return send(s_out.at[j], s_in.at[j], z_ss.at[j], z_rs.at[j], (me + GROUP) % n)

    def e_copy(j):
        return send(e_send.at[j], e_half.at[j, y], e_ss.at[j], e_rs.at[j], pair_peer)

    def fin_place(j, s):
        h0 = j * hc + c * half + y * w + s * g
        return h0 // hn, h0 % hn

    def fin_copy(j, s):
        dev, off = fin_place(j, s)
        return send(
            s_out.at[j, pl.ds(s * g, g)], fin_s.at[pl.ds(off, g)],
            f_ss.at[j, s], f_rs.at[off // g], dev,
        )

    def fin_local(j, s):
        _, off = fin_place(j, s)
        return pltpu.make_async_copy(s_out.at[j, pl.ds(s * g, g)], fin_s.at[pl.ds(off, g)], f_ls)

    def chain(j):
        pair_copy(j).wait_recv()

        @pl.when(plane > 0)
        def _():
            z_copy(j).wait_recv()

        for k in range(w):
            h = j * hc + c * half + y * w + k
            f01 = frow(0, h) * frow(1, h)
            f23 = frow(2, h) * frow(3, h)
            mine = u_mine[j, k]
            other = u_pair[j, k].astype(F32)
            entry = s_in[j, k].astype(F32)
            mid = f01 * entry + jnp.where(y == 0, mine, other)
            s_out[j, k] = (f23 * mid + jnp.where(y == 0, other, mine)).astype(BF16)
            e_send[j, k] = jnp.where(y == 0, mid, entry).astype(BF16)
            e_half[j, y, k] = jnp.where(y == 0, entry, mid).astype(BF16)

        @pl.when(plane < planes - 1)
        def _():
            z_copy(j).start()

        @pl.when(plane == planes - 1)
        def _():
            for s in range(w // g):
                dev, _off = fin_place(j, s)

                @pl.when(dev != me)
                def _():
                    fin_copy(j, s).start()

                @pl.when(dev == me)
                def _():
                    fin_local(j, s).start()
                    fin_local(j, s).wait()

    def inside(i):
        j = i // 2

        @pl.when(i % 2 == 0)
        def _():
            load(2, q_hbm, q_s, j).wait()

        ci = cumc_s[i]
        blk = tok // 2

        for t in range(half):
            at_h = pl.ds(pl.multiple_of(i * (half * D) + t * D, D), D)
            row = cumt_s[pl.ds(i * half + t, 1), :]
            scores = dot(q_s[:, at_h], k_s[:, at_h], ((1,), (1,)))
            low = ci[:blk, t:t + 1] - row[:, :blk]
            top = (scores[:blk, :blk] * jnp.exp2(low + pen_s[:blk, :blk])).astype(BF16)
            bot = (scores[blk:] * jnp.exp2((ci[blk:, t:t + 1] - row) + pen_s[blk:, :])).astype(BF16)
            top = jnp.concatenate([top, jnp.zeros_like(top)], axis=1)
            wt = jnp.concatenate([top, bot], axis=0)
            mix_s[:, at_h] = dot(wt, v_s[:, at_h], ((1,), (0,)))

    def x_copy(j):
        return send(x_send.at[j], ent.at[j, c], x_ss.at[j], x_rs.at[j], core_peer)

    def spread(j):
        e_copy(j).wait_recv()
        for yo in range(2):
            for k in range(w):
                h = j * hc + c * half + yo * w + k
                first = e_half[j, yo, k]
                u0 = jnp.where(c == 0, u_own[j, 0, yo, k], u_core[j, yo, k]).astype(F32)
                second = (frow(2 * y, h) * first.astype(F32) + u0).astype(BF16)
                ent[j, c, yo, k] = jnp.where(c == 0, first, second)
                x_send[j, yo, k] = jnp.where(c == 0, second, first)
        x_copy(j).start()

    def store(j):
        return pltpu.make_async_copy(mix_s.at[:, cols(j)], mix_hbm.at[:, cols(j)], out_sem.at[j])

    def across(j):
        x_copy(j).wait_recv()
        load(3, g_hbm, g_s, j).wait()
        lj = coef_s[j, :, 0:hc]
        acc = ssq_s[...]
        for t in range(hc):
            st = ent[j, t // half, (t % half) // w, t % w]
            mixed = mix_s[:, hcol(j, t)] + lj[:, t:t + 1] * dot(q_s[:, hcol(j, t)], st, ((1,), (0,)))
            acc = acc + mixed * mixed
            gate = g_s[:, hcol(j, t)].astype(F32)
            mix_s[:, hcol(j, t)] = mixed * (gain_ref[:, hcol(j, t)] * jax.nn.sigmoid(gate))
        ssq_s[...] = acc
        store(j).start()

    def fac_copy(d):
        return send(fac_own, fac_s.at[r], fac_ss.at[d - 1], fac_rs.at[d - 1], plane * GROUP + (r + d) % GROUP)

    updates(0)
    pl.semaphore_wait(barrier, n - 1)
    for d in range(1, GROUP):
        fac_copy(d).start()
    core_copy(0).start()
    ssq_s[...] = jnp.zeros_like(ssq_s)
    updates(1)
    core_copy(1).start()
    for d in range(1, GROUP):
        fac_copy(d).wait_recv()
    combine(0)

    chain_lag = CHAIN_LAG + HOP_LAG * plane
    e_lag = CHAIN_LAG + HOP_LAG * (planes - 1)
    spread_lag = e_lag + E_LAG
    across_lag = spread_lag + X_LAG
    steps = max(chunks + across_lag, 2 * chunks + INSIDE_LAG)

    def step(t, carry):
        def at(lag, count, body):
            @pl.when((t >= lag) & (t < lag + count))
            def _():
                body(t - lag)

        def first(j):
            updates(j)
            core_copy(j).start()

        at(1, chunks, combine)
        at(chain_lag, chunks, chain)
        at(e_lag, chunks, lambda j: e_copy(j).start())
        at(spread_lag, chunks, spread)
        at(0, chunks, first)
        at(INSIDE_LAG, 2 * chunks, inside)
        at(across_lag, chunks, across)
        return carry

    lax.fori_loop(2, steps, step, 0)

    total = jnp.sum(ssq_s[...], axis=1, keepdims=True) * (1.0 / (heads * D))
    ssq_s[...] = jnp.broadcast_to(lax.rsqrt(total + EPS), (tok, D))

    for s in range(hn // g):
        h0 = me * hn + s * g
        pos = h0 % hc
        src = (planes - 1) * GROUP + ((pos % half) // w) * 2 + pos // half

        @pl.when(src != me)
        def _():
            send(
                s_out.at[0, pl.ds(0, g)], fin_s.at[pl.ds(s * g, g)], f_ss.at[0, 0], f_rs.at[s], core_peer
            ).wait_recv()

    for d in range(1, GROUP):
        fac_copy(d).wait_send()

    def drain(j, carry):
        core_copy(j).wait_send()
        pair_copy(j).wait_send()
        e_copy(j).wait_send()
        x_copy(j).wait_send()
        store(j).wait()

        @pl.when(plane < planes - 1)
        def _():
            z_copy(j).wait_send()

        @pl.when(plane == planes - 1)
        def _():
            for s in range(w // g):
                dev, _off = fin_place(j, s)

                @pl.when(dev != me)
                def _():
                    fin_copy(j, s).wait_send()

        return carry

    lax.fori_loop(0, chunks, drain, 0)


def finish_kernel(mix_ref, inv_ref, fin_in, out_ref, fin_ref):
    inv = inv_ref[...]
    for t in range(mix_ref.shape[1] // D):
        at = slice(t * D, (t + 1) * D)
        out_ref[:, at] = (mix_ref[:, at] * inv).astype(BF16)
    fin_ref[...] = fin_in[...].astype(F32)


def shards(n, queries, keys_in, values_in, log_decay, gate_logits, norm_gain, doc_lengths):
    tok, width = queries.shape
    heads = width // D
    chunks = CHUNKS
    hc = heads // chunks
    half = hc // 2
    w = half // 2
    hn = heads // n
    g = math.gcd(w, hn)
    vm = pltpu.VMEM
    dma = pltpu.SemaphoreType.DMA
    anyspace = pl.BlockSpec(memory_space=pl.ANY)
    vspec = pl.BlockSpec(memory_space=pltpu.VMEM)
    part = vm((chunks, w, D, D), BF16)
    scratch = [
        vm((tok, width), F32),
        vm((tok, width), BF16), vm((tok, width), BF16), vm((tok, width), BF16), vm((tok, width), BF16),
        vm((tok, tok), F32),
        vm((heads, tok), F32), vm((2 * chunks, tok, half), F32), vm((chunks, tok, 2 * hc), F32),
        vm((heads, D), F32), vm((GROUP, heads, D), F32),
        vm((chunks, 2, 2, w, D, D), BF16), vm((chunks, 2, w, D, D), BF16), vm((chunks, w, D, D), F32),
        part, part, part, part, part,
        vm((chunks, 2, w, D, D), BF16), vm((chunks, 2, w, D, D), BF16),
        vm((chunks, 2, 2, w, D, D), BF16),
        dma((4, chunks)), dma((chunks,)), dma((GROUP - 1,)), dma((GROUP - 1,)),
        dma((chunks,)), dma((chunks,)), dma((chunks,)), dma((chunks,)), dma((chunks,)), dma((chunks,)),
        dma((chunks,)), dma((chunks,)), dma((chunks,)), dma((chunks,)),
        dma((chunks, w // g)), dma((hn // g,)), dma,
    ]
    mixed, squares, final = pl.pallas_call(
        functools.partial(kernel, n, heads, chunks),
        out_shape=(
            jax.ShapeDtypeStruct((tok, width), F32),
            jax.ShapeDtypeStruct((tok, D), F32),
            jax.ShapeDtypeStruct((hn, D, D), BF16),
        ),
        in_specs=[anyspace] * 4 + [vspec, vspec, pl.BlockSpec(memory_space=pltpu.SMEM)],
        out_specs=(anyspace, vspec, vspec),
        scratch_shapes=scratch,
        compiler_params=pltpu.CompilerParams(
            collective_id=0, has_side_effects=True, vmem_limit_bytes=60 * 1024 * 1024
        ),
    )(queries, keys_in, values_in, gate_logits, log_decay.T, norm_gain.reshape(1, width), doc_lengths)
    rows = tok // FINISH_PARTS
    return pl.pallas_call(
        finish_kernel,
        out_shape=(
            jax.ShapeDtypeStruct((tok, width), BF16),
            jax.ShapeDtypeStruct((hn, D, D), F32),
        ),
        grid=(FINISH_PARTS,),
        in_specs=[
            pl.BlockSpec((rows, width), lambda i: (i, 0)),
            pl.BlockSpec((rows, D), lambda i: (i, 0)),
            pl.BlockSpec((hn, D, D), lambda i: (0, 0, 0)),
        ],
        out_specs=(
            pl.BlockSpec((rows, width), lambda i: (i, 0)),
            pl.BlockSpec((hn, D, D), lambda i: (0, 0, 0)),
        ),
        compiler_params=pltpu.CompilerParams(vmem_limit_bytes=60 * 1024 * 1024),
    )(mixed, squares, final)


def solution(mesh):
    rows = P(("grp", "seq"), None)
    return jax.shard_map(
        functools.partial(shards, mesh.shape["seq"]),
        mesh=mesh,
        in_specs=(rows, rows, rows, rows, rows, P(), P("grp")),
        out_specs=(rows, P(("grp", "seq"), None, None)),
        check_vma=False,
    )
```

```python
import functools
import math

import jax
import jax.numpy as jnp
from jax import lax
from jax.experimental import pallas as pl
from jax.experimental.pallas import tpu as pltpu
from jax.sharding import PartitionSpec as P

EPS = 1e-05
LOG2E = 1.4426950408889634
D = 128
GROUP = 4
CHUNKS = 8
INSIDE_LAG = 2
CHAIN_LAG = 4
HOP_LAG = 2
E_LAG = 4
X_LAG = 2
FINISH_PARTS = 2
F32, BF16 = jnp.float32, jnp.bfloat16
MESH = pl.DeviceIdType.MESH


def dot(a, b, dims):
    return lax.dot_general(a, b, (dims, ((), ())), preferred_element_type=F32)


def kernel(
    n, heads, chunks,
    q_hbm, k_hbm, v_hbm, g_hbm, ld_ref, gain_ref, docs_ref,
    mix_hbm, ssq_s, fin_s,
    mix_s, q_s, k_s, v_s, g_s, pen_s, cumt_s, cumc_s, coef_s,
    fac_own, fac_s, u_own, u_core, u_mine, u_send, u_pair, s_in, s_out, e_send, e_half, x_send, ent,
    load_sem, out_sem, fac_ss, fac_rs, core_ss, core_rs, pair_ss, pair_rs, z_ss, z_rs, e_ss, e_rs,
    x_ss, x_rs, f_ss, f_rs, f_ls,
):
    tok = q_hbm.shape[0]
    hc = heads // chunks
    half = hc // 2
    w = half // 2
    planes = n // GROUP
    hn = heads // n
    g = math.gcd(w, hn)
    me = lax.axis_index("seq")
    plane = me // GROUP
    r = me % GROUP
    y = r // 2
    c = r % 2
    core_peer = plane * GROUP + y * 2 + (1 - c)
    pair_peer = plane * GROUP + (1 - y) * 2 + c

    def send(src, dst, ss, rs, dev):
        return pltpu.make_async_remote_copy(
            src_ref=src, dst_ref=dst, send_sem=ss, recv_sem=rs,
            device_id={"seq": dev}, device_id_type=MESH,
        )

    barrier = pltpu.get_barrier_semaphore()

    def greet(i, carry):
        pl.semaphore_signal(barrier, inc=1, device_id={"seq": (me + i) % n}, device_id_type=MESH)
        return carry

    lax.fori_loop(1, n, greet, 0)

    def cols(j):
        return pl.ds(pl.multiple_of(j * (hc * D), hc * D), hc * D)

    def load(which, hbm, vm, j):
        return pltpu.make_async_copy(hbm.at[:, cols(j)], vm.at[:, cols(j)], load_sem.at[which, j])

    loads = ((k_hbm, k_s), (v_hbm, v_s), (q_hbm, q_s), (g_hbm, g_s))

    def start_kv(j, carry):
        load(0, k_hbm, k_s, j).start()
        load(1, v_hbm, v_s, j).start()
        return carry

    def start_qg(j, carry):
        load(2, q_hbm, q_s, j).start()
        load(3, g_hbm, g_s, j).start()
        return carry

    lax.fori_loop(0, chunks, start_kv, 0)
    lax.fori_loop(0, chunks, start_qg, 0)

    n_docs = docs_ref.shape[0]
    rows = lax.broadcasted_iota(jnp.int32, (tok, D), 0)
    lanes = lax.broadcasted_iota(jnp.int32, (1, tok), 1)
    base = me * tok
    doc_col = jnp.zeros((tok, D), jnp.int32)
    doc_row = jnp.zeros((1, tok), jnp.int32)
    before = jnp.int32(0)
    last = jnp.int32(0)
    end = jnp.int32(0)
    for d in range(n_docs):
        end = end + docs_ref[d]
        doc_col = doc_col + jnp.where(rows + base >= end, 1, 0)
        doc_row = doc_row + jnp.where(lanes + base >= end, 1, 0)
        before = before + jnp.where(base - 1 >= end, 1, 0)
        last = last + jnp.where(base + tok - 1 >= end, 1, 0)
    causal = lax.broadcasted_iota(jnp.int32, (tok, tok), 0) >= lax.broadcasted_iota(jnp.int32, (tok, tok), 1)
    pen_s[...] = jnp.where(causal & (doc_col[:, :1] == doc_row), 0.0, -1e30).astype(F32)
    tri = jnp.where(causal, 1.0, 0.0).astype(BF16)
    ld = ld_ref[...]
    cum = dot(tri, ld, ((1,), (1,)))
    cumt = dot(ld, tri, ((1,), (1,)))
    cumt_s[...] = LOG2E * cumt
    carried = jnp.where(doc_col[:, :heads] == before, 1.0, 0.0).astype(F32)
    closing = jnp.where(doc_col[:, :heads] == last, 1.0, 0.0).astype(F32)
    lead = carried * jnp.exp(cum)
    kw = closing * jnp.exp(cum[tok - 1:tok, :] - cum)
    for j in range(chunks):
        at = slice(j * hc, (j + 1) * hc)
        coef_s[j, :, 0:hc] = lead[:, at]
        coef_s[j, :, hc:2 * hc] = kw[:, at]
    for i in range(2 * chunks):
        cumc_s[i] = LOG2E * cum[:, i * half:(i + 1) * half]
    own_f = jnp.where(last == before, 1.0, 0.0).astype(F32) * jnp.exp(
        jnp.broadcast_to(cumt[:, tok - 1:tok], (heads, D))
    )
    fac_own[...] = own_f
    fac_s[r] = own_f

    @pl.when(plane == 0)
    def _():
        s_in[...] = jnp.zeros_like(s_in)

    def lane(t):
        return slice(t * D, (t + 1) * D)

    def hcol(j, t):
        return pl.ds(pl.multiple_of(j * (hc * D) + t * D, D), D)

    def updates(j):
        load(0, k_hbm, k_s, j).wait()
        load(1, v_hbm, v_s, j).wait()
        kwj = coef_s[j, :, hc:2 * hc]
        for t in range(hc):
            kk = k_s[:, hcol(j, t)].astype(F32)
            wk = (kk * kwj[:, t:t + 1]).astype(BF16)
            up = dot(wk, v_s[:, hcol(j, t)], ((0,), (0,)))
            u_own[j, t // half, (t % half) // w, t % w] = up.astype(BF16)

    def frow(slot, h):
        return fac_s[slot, pl.ds(h, 1), :]

    def core_copy(j):
        return send(u_own.at[j, 1 - c], u_core.at[j], core_ss.at[j], core_rs.at[j], core_peer)

    def pair_copy(j):
        return send(u_send.at[j], u_pair.at[j], pair_ss.at[j], pair_rs.at[j], pair_peer)

    def combine(j):
        core_copy(j).wait_recv()
        for k in range(w):
            for mine in (True, False):
                yo = y if mine else 1 - y
                h = j * hc + c * half + yo * w + k
                f1 = frow(2 * y + 1, h)
                fa = jnp.where(c == 0, f1, 1.0)
                fb = jnp.where(c == 0, 1.0, f1)
                val = fa * u_own[j, c, yo, k].astype(F32) + fb * u_core[j, yo, k].astype(F32)
                if mine:
                    u_mine[j, k] = val
                else:
                    u_send[j, k] = val.astype(BF16)
        pair_copy(j).start()

    def z_copy(j):
        return send(s_out.at[j], s_in.at[j], z_ss.at[j], z_rs.at[j], (me + GROUP) % n)

    def e_copy(j):
        return send(e_send.at[j], e_half.at[j, y], e_ss.at[j], e_rs.at[j], pair_peer)

    def fin_place(j, s):
        h0 = j * hc + c * half + y * w + s * g
        return h0 // hn, h0 % hn

    def fin_copy(j, s):
        dev, off = fin_place(j, s)
        return send(
            s_out.at[j, pl.ds(s * g, g)], fin_s.at[pl.ds(off, g)],
            f_ss.at[j, s], f_rs.at[off // g], dev,
        )

    def fin_local(j, s):
        _, off = fin_place(j, s)
        return pltpu.make_async_copy(s_out.at[j, pl.ds(s * g, g)], fin_s.at[pl.ds(off, g)], f_ls)

    def chain(j):
        pair_copy(j).wait_recv()

        @pl.when(plane > 0)
        def _():
            z_copy(j).wait_recv()

        for k in range(w):
            h = j * hc + c * half + y * w + k
            f01 = frow(0, h) * frow(1, h)
            f23 = frow(2, h) * frow(3, h)
            mine = u_mine[j, k]
            other = u_pair[j, k].astype(F32)
            entry = s_in[j, k].astype(F32)
            mid = f01 * entry + jnp.where(y == 0, mine, other)
            s_out[j, k] = (f23 * mid + jnp.where(y == 0, other, mine)).astype(BF16)
            e_send[j, k] = jnp.where(y == 0, mid, entry).astype(BF16)
            e_half[j, y, k] = jnp.where(y == 0, entry, mid).astype(BF16)

        @pl.when(plane < planes - 1)
        def _():
            z_copy(j).start()

        @pl.when(plane == planes - 1)
        def _():
            for s in range(w // g):
                dev, _off = fin_place(j, s)

                @pl.when(dev != me)
                def _():
                    fin_copy(j, s).start()

                @pl.when(dev == me)
                def _():
                    fin_local(j, s).start()
                    fin_local(j, s).wait()

    def inside(i):
        j = i // 2

        @pl.when(i % 2 == 0)
        def _():
            load(2, q_hbm, q_s, j).wait()

        ci = cumc_s[i]
        blk = tok // 2

        for t in range(half):
            at_h = pl.ds(pl.multiple_of(i * (half * D) + t * D, D), D)
            row = cumt_s[pl.ds(i * half + t, 1), :]
            scores = dot(q_s[:, at_h], k_s[:, at_h], ((1,), (1,)))
            low = ci[:blk, t:t + 1] - row[:, :blk]
            top = (scores[:blk, :blk] * jnp.exp2(low + pen_s[:blk, :blk])).astype(BF16)
            bot = (scores[blk:] * jnp.exp2((ci[blk:, t:t + 1] - row) + pen_s[blk:, :])).astype(BF16)
            top = jnp.concatenate([top, jnp.zeros_like(top)], axis=1)
            wt = jnp.concatenate([top, bot], axis=0)
            mix_s[:, at_h] = dot(wt, v_s[:, at_h], ((1,), (0,)))

    def x_copy(j):
        return send(x_send.at[j], ent.at[j, c], x_ss.at[j], x_rs.at[j], core_peer)

    def spread(j):
        e_copy(j).wait_recv()
        for yo in range(2):
            for k in range(w):
                h = j * hc + c * half + yo * w + k
                first = e_half[j, yo, k]
                u0 = jnp.where(c == 0, u_own[j, 0, yo, k], u_core[j, yo, k]).astype(F32)
                second = (frow(2 * y, h) * first.astype(F32) + u0).astype(BF16)
                ent[j, c, yo, k] = jnp.where(c == 0, first, second)
                x_send[j, yo, k] = jnp.where(c == 0, second, first)
        x_copy(j).start()

    def store(j):
        return pltpu.make_async_copy(g_s.at[:, cols(j)], mix_hbm.at[:, cols(j)], out_sem.at[j])

    def across(j):
        x_copy(j).wait_recv()
        load(3, g_hbm, g_s, j).wait()
        lj = coef_s[j, :, 0:hc]
        acc = ssq_s[...]
        for t in range(hc):
            st = ent[j, t // half, (t % half) // w, t % w]
            mixed = mix_s[:, hcol(j, t)] + lj[:, t:t + 1] * dot(q_s[:, hcol(j, t)], st, ((1,), (0,)))
            acc = acc + mixed * mixed
            gate = g_s[:, hcol(j, t)].astype(F32)
            g_s[:, hcol(j, t)] = (mixed * (gain_ref[:, hcol(j, t)] * (0.5 * jnp.tanh(0.5 * gate) + 0.5))).astype(BF16)
        ssq_s[...] = acc
        store(j).start()

    def fac_copy(d):
        return send(fac_own, fac_s.at[r], fac_ss.at[d - 1], fac_rs.at[d - 1], plane * GROUP + (r + d) % GROUP)

    updates(0)
    pl.semaphore_wait(barrier, n - 1)
    for d in range(1, GROUP):
        fac_copy(d).start()
    core_copy(0).start()
    ssq_s[...] = jnp.zeros_like(ssq_s)
    updates(1)
    core_copy(1).start()
    for d in range(1, GROUP):
        fac_copy(d).wait_recv()
    combine(0)

    chain_lag = CHAIN_LAG + HOP_LAG * plane
    e_lag = CHAIN_LAG + HOP_LAG * (planes - 1)
    spread_lag = e_lag + E_LAG
    across_lag = spread_lag + X_LAG
    steps = max(chunks + across_lag, 2 * chunks + INSIDE_LAG)

    def step(t, carry):
        def at(lag, count, body):
            @pl.when((t >= lag) & (t < lag + count))
            def _():
                body(t - lag)

        def first(j):
            updates(j)
            core_copy(j).start()

        at(1, chunks, combine)
        at(chain_lag, chunks, chain)
        at(e_lag, chunks, lambda j: e_copy(j).start())
        at(spread_lag, chunks, spread)
        at(0, chunks, first)
        at(INSIDE_LAG, 2 * chunks, inside)
        at(across_lag, chunks, across)
        return carry

    lax.fori_loop(2, steps, step, 0)

    total = jnp.sum(ssq_s[...], axis=1, keepdims=True) * (1.0 / (heads * D))
    ssq_s[...] = jnp.broadcast_to(lax.rsqrt(total + EPS), (tok, D))

    for s in range(hn // g):
        h0 = me * hn + s * g
        pos = h0 % hc
        src = (planes - 1) * GROUP + ((pos % half) // w) * 2 + pos // half

        @pl.when(src != me)
        def _():
            send(
                s_out.at[0, pl.ds(0, g)], fin_s.at[pl.ds(s * g, g)], f_ss.at[0, 0], f_rs.at[s], core_peer
            ).wait_recv()

    for d in range(1, GROUP):
        fac_copy(d).wait_send()

    def drain(j, carry):
        core_copy(j).wait_send()
        pair_copy(j).wait_send()
        e_copy(j).wait_send()
        x_copy(j).wait_send()
        store(j).wait()

        @pl.when(plane < planes - 1)
        def _():
            z_copy(j).wait_send()

        @pl.when(plane == planes - 1)
        def _():
            for s in range(w // g):
                dev, _off = fin_place(j, s)

                @pl.when(dev != me)
                def _():
                    fin_copy(j, s).wait_send()

        return carry

    lax.fori_loop(0, chunks, drain, 0)


def finish_kernel(mix_ref, inv_ref, fin_in, out_ref, fin_ref):
    inv = inv_ref[...]
    for t in range(mix_ref.shape[1] // D):
        at = slice(t * D, (t + 1) * D)
        out_ref[:, at] = (mix_ref[:, at].astype(F32) * inv).astype(BF16)
    fin_ref[...] = fin_in[...].astype(F32)


def shards(n, queries, keys_in, values_in, log_decay, gate_logits, norm_gain, doc_lengths):
    tok, width = queries.shape
    heads = width // D
    chunks = CHUNKS
    hc = heads // chunks
    half = hc // 2
    w = half // 2
    hn = heads // n
    g = math.gcd(w, hn)
    vm = pltpu.VMEM
    dma = pltpu.SemaphoreType.DMA
    anyspace = pl.BlockSpec(memory_space=pl.ANY)
    vspec = pl.BlockSpec(memory_space=pltpu.VMEM)
    part = vm((chunks, w, D, D), BF16)
    scratch = [
        vm((tok, width), F32),
        vm((tok, width), BF16), vm((tok, width), BF16), vm((tok, width), BF16), vm((tok, width), BF16),
        vm((tok, tok), F32),
        vm((heads, tok), F32), vm((2 * chunks, tok, half), F32), vm((chunks, tok, 2 * hc), F32),
        vm((heads, D), F32), vm((GROUP, heads, D), F32),
        vm((chunks, 2, 2, w, D, D), BF16), vm((chunks, 2, w, D, D), BF16), vm((chunks, w, D, D), F32),
        part, part, part, part, part,
        vm((chunks, 2, w, D, D), BF16), vm((chunks, 2, w, D, D), BF16),
        vm((chunks, 2, 2, w, D, D), BF16),
        dma((4, chunks)), dma((chunks,)), dma((GROUP - 1,)), dma((GROUP - 1,)),
        dma((chunks,)), dma((chunks,)), dma((chunks,)), dma((chunks,)), dma((chunks,)), dma((chunks,)),
        dma((chunks,)), dma((chunks,)), dma((chunks,)), dma((chunks,)),
        dma((chunks, w // g)), dma((hn // g,)), dma,
    ]
    mixed, squares, final = pl.pallas_call(
        functools.partial(kernel, n, heads, chunks),
        out_shape=(
            jax.ShapeDtypeStruct((tok, width), BF16),
            jax.ShapeDtypeStruct((tok, D), F32),
            jax.ShapeDtypeStruct((hn, D, D), BF16),
        ),
        in_specs=[anyspace] * 4 + [vspec, vspec, pl.BlockSpec(memory_space=pltpu.SMEM)],
        out_specs=(anyspace, vspec, vspec),
        scratch_shapes=scratch,
        compiler_params=pltpu.CompilerParams(
            collective_id=0, has_side_effects=True, vmem_limit_bytes=60 * 1024 * 1024
        ),
    )(queries, keys_in, values_in, gate_logits, log_decay.T, norm_gain.reshape(1, width), doc_lengths)
    rows = tok // FINISH_PARTS
    return pl.pallas_call(
        finish_kernel,
        out_shape=(
            jax.ShapeDtypeStruct((tok, width), BF16),
            jax.ShapeDtypeStruct((hn, D, D), F32),
        ),
        grid=(FINISH_PARTS,),
        in_specs=[
            pl.BlockSpec((rows, width), lambda i: (i, 0)),
            pl.BlockSpec((rows, D), lambda i: (i, 0)),
            pl.BlockSpec((hn, D, D), lambda i: (0, 0, 0)),
        ],
        out_specs=(
            pl.BlockSpec((rows, width), lambda i: (i, 0)),
            pl.BlockSpec((hn, D, D), lambda i: (0, 0, 0)),
        ),
        compiler_params=pltpu.CompilerParams(vmem_limit_bytes=60 * 1024 * 1024),
    )(mixed, squares, final)


def solution(mesh):
    rows = P(("grp", "seq"), None)
    return jax.shard_map(
        functools.partial(shards, mesh.shape["seq"]),
        mesh=mesh,
        in_specs=(rows, rows, rows, rows, rows, P(), P("grp")),
        out_specs=(rows, P(("grp", "seq"), None, None)),
        check_vma=False,
    )
```
